32 devices in a mesh: row: 4 (over x, core), col: 8 (over z, y).
Axes of the slice: x: 2, y: 2, z: 4, core: 2. Of those that a mesh axis runs over, the one named last changes fastest.
Arguments:
- amplitudes: bfloat16 [16384, 4096], P(('row', 'col')), may hold values from -6 to 6
- live_tiles: int32 [256, 32], P(('row', 'col')), may hold values 0 or 1
- destination: int32 [256], P(('row', 'col')), may hold values from 0 to 255, as said below
- integral_list: int32 [32, 2], replicated, may hold values from 0 to 31, as said below
- integral_tiles: bfloat16 [32, 128, 128], P(('row', 'col')), may hold values from -0.25 to 0.25
Outputs:
- ladder: bfloat16 [16384, 1024], P(('row', 'col'))
The draws below stay inside these ranges and needn't reach their ends.
Inputs may be any that keep to these rules, and one draw needn't show every extreme that they name: destination is a permutation of the pair tiles that keeps each tile within its row group (8 consecutive devices in row+col order); of one device's 8 stored tiles at most 2 have their output on any one device, and some device reaches 2 in every draw. `integral_list`: the (c, d) tile comes first and is below 32, the (a, b) tile second and below 8; no pair of tiles is listed twice.
All inputs are finite; a program needn't handle non-finite values. No bound on the sum of `live_tiles` on one device may be relied on, other than what follows from the above.
Results may differ from the reference program's by a relative error of at most 0.001.
Values may be sent and summed in bfloat16 or wider, within the bound.
No kernel may reach another device: no remote copies, remote signals or barrier semaphores. Data moves between devices by JAX's collectives and lax.ppermute only.
A program may use at most 192 MiB of HBM per device.

```python
import jax
import jax.numpy as jnp
from jax import lax

TILE = 128
KT = 32
AT = 8
PT = 64
NXT = 256
NX = 16384
VNZ = 32
N_ROW = 4
N_COL = 8


def draw_destination(key, part):

    def shuffle_one(slot_key):
        return jax.random.permutation(slot_key, N_COL).astype(jnp.int32)

    def one_row(row_key, row_number):
        first_key, slot_key, place_key = jax.random.split(row_key, 3)
        sigma = jax.random.permutation(first_key, N_COL).astype(jnp.int32)
        sigma_next = jnp.roll(sigma, -1)
        column_ids = jnp.arange(N_COL, dtype=jnp.int32)
        targets = jnp.where(column_ids[None, :] == sigma_next[:, None], sigma[:, None], column_ids[None, :])
        shuffles = jax.vmap(shuffle_one)(jax.random.split(slot_key, N_COL))
        targets = jnp.take_along_axis(targets, shuffles, axis=1)
        flat_targets = targets.reshape(-1)
        tie_break = jax.random.permutation(place_key, N_COL * N_COL).astype(jnp.int32)
        sort_keys = flat_targets * (N_COL * N_COL) + tie_break
        sorted_order = jnp.argsort(sort_keys, stable=True)
        ranks = jnp.zeros((N_COL * N_COL,), jnp.int32).at[sorted_order].set(jnp.arange(N_COL * N_COL, dtype=jnp.int32))
        positions = ranks - flat_targets * N_COL
        return (row_number * N_COL + flat_targets) * N_COL + positions
    row_keys = jax.random.split(jax.random.fold_in(key, 11), N_ROW)
    result = jax.vmap(one_row)(row_keys, jnp.arange(N_ROW, dtype=jnp.int32))
    return result.reshape(-1).astype(jnp.int32)


def draw_integral_list(key, part):
    chosen = jax.random.permutation(jax.random.fold_in(key, 5), KT * AT)[:VNZ].astype(jnp.int32)
    return jnp.stack([chosen // AT, chosen % AT], axis=1).astype(jnp.int32)


def plant(array, key, smallest, largest):
    spot = [jax.random.randint(jax.random.fold_in(key, axis), (), 0, length) for axis, length in enumerate(array.shape)]
    widest = array.shape.index(max(array.shape))
    beside = spot[:widest] + [(spot[widest] + 1) % array.shape[widest]] + spot[widest + 1:]
    return array.at[tuple(spot)].set(smallest).at[tuple(beside)].set(largest)


def block_scale(rng, shape, shards, smallest, high):
    def one(position, blocks):
        draws = jax.random.uniform(jax.random.fold_in(jax.random.fold_in(rng, 6), position), (blocks,), jnp.float32, smallest / len(shards), high / len(shards))
        return jnp.repeat(jnp.exp(draws), shape[position] // blocks).reshape((-1,) + (1,) * (len(shape) - position - 1))

    level = one(*shards[0])
    for cut in shards[1:]:
        level = level * one(*cut)
    return level


def scatter_about(stream_key, shape, deviation, bound, cuts=(), kind=jnp.bfloat16):
    loudness = block_scale(stream_key, shape, cuts, -0.22, 0.18) if cuts else 1.0
    values = jax.random.normal(stream_key, shape, jnp.float32) * deviation * loudness
    return jnp.minimum(jnp.maximum(values, -bound), bound).astype(kind)


def setup_inputs(seed: int = 0) -> dict:
    seeds = jax.random.split(jax.random.key(seed), 6)
    return {
        "amplitudes": scatter_about(seeds[0], (NX, KT * TILE), 1.0, 6.0, ((0, 32),)),
        "live_tiles": plant((jax.random.randint(seeds[1], (NXT, KT), 0, 4) < 3).astype(jnp.int32), jax.random.fold_in(seeds[1], 1), 0, 1),
        "destination": draw_destination(jax.random.fold_in(seeds[5], 71), 0),
        "integral_list": draw_integral_list(jax.random.fold_in(seeds[5], 71), 0),
        "integral_tiles": scatter_about(seeds[4], (VNZ, TILE, TILE), (TILE * VNZ // AT) ** -0.5, 0.25, ((0, 32),)),
    }


def reference(amplitudes, live_tiles, destination, integral_list, integral_tiles):
    blocks = jnp.zeros((KT, AT, TILE, TILE), integral_tiles.dtype)
    blocks = blocks.at[integral_list[:, 0], integral_list[:, 1]].set(integral_tiles)
    integrals = blocks.transpose(0, 2, 1, 3).reshape(KT * TILE, AT * TILE)
    stored = amplitudes.reshape(NXT, PT, KT, TILE)
    inverse = jnp.zeros((NXT,), jnp.int32).at[destination].set(jnp.arange(NXT, dtype=jnp.int32))

    def one_group(indices):
        tile_rows = stored[indices] * live_tiles[indices][:, None, :, None].astype(amplitudes.dtype)
        tile_rows = tile_rows.reshape(-1, KT * TILE)
        return jnp.dot(tile_rows, integrals, preferred_element_type=jnp.float32).astype(jnp.bfloat16)

    groups = lax.map(one_group, inverse.reshape(NXT // N_COL, N_COL))
    return groups.reshape(NXT * PT, AT * TILE)
```

```python
import functools

import jax
import jax.numpy as jnp
from jax import lax
from jax.experimental import pallas as pl
from jax.experimental.pallas import tpu as pltpu
from jax.sharding import PartitionSpec as P

AT = 8
META = 16


VMEM = pl.BlockSpec(memory_space=pltpu.VMEM)
SMEM = pl.BlockSpec(memory_space=pltpu.SMEM)
ANY = pl.BlockSpec(memory_space=pl.ANY)


def swap(value, mask, sizes):
    rows, cols = sizes
    pairs = [
        (r * cols + c, (r ^ mask[0]) * cols + (c ^ mask[1]))
        for r in range(rows)
        for c in range(cols)
    ]
    return lax.ppermute(value, ("row", "col"), pairs)


def gather_all(block, sizes):
    rows, cols = sizes
    step = cols // 4
    far = [(0, m * step) for m in range(4)]
    near = [(2 * i, j) for i in range(rows // 2) for j in range(step)]
    order = sorted(range(1, 4), key=lambda m: m != 2)
    pieces = {0: block}
    for m in order:
        pieces[m] = swap(block, far[m], sizes)
    line = jnp.concatenate([pieces[m] for m in range(4)], axis=0)
    parts = [line]
    for mask in reversed(near[1:]):
        parts.append(swap(line, mask, sizes))
    masks = [near[0]] + list(reversed(near[1:]))
    mine = jnp.concatenate(parts, axis=0)
    other = swap(mine, (1, 0), sizes)
    held = [(a[0] ^ b[0], a[1] ^ b[1]) for a in masks for b in far]
    held = held + [(a ^ 1, b) for a, b in held]
    return mine, other, held


def contract_kernel(pair_rows, inner_tiles, unroll, places, devices, live, source, amp, mine, other, *rest):
    outs, total = rest[:-1], rest[-1]
    half = mine.shape[0]
    width = mine.shape[2]
    tiles = amp.shape[0] // pair_rows
    total[...] = jnp.zeros_like(total)

    def add_tiles(ref, base):
        def step(q, carry):
            entry = devices[base + q]
            k, a = places[2 * entry], places[2 * entry + 1]
            inner = pl.ds(pl.multiple_of(k * width, width), width)
            outer = pl.ds(pl.multiple_of(a * width, width), width)
            parts = []
            for s in range(tiles):
                part = amp[s * pair_rows : (s + 1) * pair_rows, inner]
                alive = live[s * inner_tiles + k] != 0
                parts.append(jnp.where(alive, part, jnp.zeros_like(part)))
            left = jnp.concatenate(parts, axis=0)
            right = ref[q, pl.ds(0, width), :]
            total[:, outer] += jnp.dot(left, right, preferred_element_type=jnp.float32)
            return carry

        lax.fori_loop(0, half, step, 0, unroll=min(unroll, half))

    add_tiles(mine, 0)
    add_tiles(other, half)
    for n, out in enumerate(outs):
        start = pl.multiple_of(source[n] * pair_rows, pair_rows)
        out[...] = total[pl.ds(start, pair_rows), :].astype(out.dtype)


def contract(places, devices, live, source, amp, mine, other, count, pair_rows, inner_tiles):
    width = mine.shape[2]
    body = functools.partial(contract_kernel, pair_rows, inner_tiles, 16)
    return pl.pallas_call(
        body,
        out_shape=[jax.ShapeDtypeStruct((pair_rows, AT * width), amp.dtype)] * count,
        in_specs=[SMEM] * 4 + [VMEM] * 3,
        out_specs=[VMEM] * count,
        scratch_shapes=[pltpu.VMEM((amp.shape[0], AT * width), jnp.float32)],
        compiler_params=pltpu.CompilerParams(vmem_limit_bytes=40 * 1024 * 1024),
        name="contract",
    )(places, devices, live, source, amp, mine, other)


def place_kernel(count, positions, *rest):
    sources, out, buffers, arrived, left = rest[:count], *rest[count:]
    rows = buffers.shape[1]

    def fetch(n):
        return pltpu.make_async_copy(sources[n], buffers.at[n], arrived.at[n])

    def store(n):
        start = pl.multiple_of(jnp.maximum(positions[n], 0) * rows, rows)
        return pltpu.make_async_copy(buffers.at[n], out.at[pl.ds(start, rows), :], left.at[n])

    for n in range(count):
        pl.when(positions[n] >= 0)(lambda n=n: fetch(n).start())
    for n in range(count):

        @pl.when(positions[n] >= 0)
        def _(n=n):
            fetch(n).wait()
            store(n).start()

    for n in range(count):
        pl.when(positions[n] >= 0)(lambda n=n: store(n).wait())


def place(positions, sources, tile_count):
    rows, width = sources[0].shape
    count = len(sources)
    return pl.pallas_call(
        functools.partial(place_kernel, count),
        out_shape=jax.ShapeDtypeStruct((tile_count * rows, width), sources[0].dtype),
        in_specs=[SMEM] + [ANY] * count,
        out_specs=ANY,
        scratch_shapes=[
            pltpu.VMEM((count, rows, width), sources[0].dtype),
            pltpu.SemaphoreType.DMA((count,)),
            pltpu.SemaphoreType.DMA((count,)),
        ],
        name="place",
    )(positions, *sources)


def nth(matches, n):
    size = matches.shape[-1]
    index = jnp.arange(size, dtype=jnp.int32)
    earlier = index[None, :] < index[:, None]
    rank = jnp.sum(jnp.logical_and(matches[..., None, :], earlier), axis=-1)
    chosen = jnp.logical_and(matches, rank == n)
    return jnp.sum(jnp.where(chosen, index, 0), axis=-1), jnp.any(chosen, axis=-1)


def shards(sizes, amplitudes, live_tiles, destination, integral_list, integral_tiles):
    rows, cols = sizes
    tile_count = destination.shape[0]
    pair_rows = amplitudes.shape[0] // tile_count
    inner_tiles = live_tiles.shape[1]
    held_tiles, width, _ = integral_tiles.shape
    my_row, my_col = lax.axis_index("row"), lax.axis_index("col")
    peers = jnp.arange(cols, dtype=jnp.int32)

    to_col = destination // tile_count % cols
    to_place = destination % tile_count
    meta = jnp.stack([to_col, to_place]).astype(integral_tiles.dtype)
    meta = jnp.pad(meta, ((0, META - 2), (0, width - tile_count)))
    meta = jnp.broadcast_to(meta[None], (held_tiles, META, width))
    block = jnp.concatenate([integral_tiles, meta], axis=1)
    mine, other, held = gather_all(block, sizes)

    row_masks = jnp.array([m[0] for m in held], dtype=jnp.int32)
    col_masks = jnp.array([m[1] for m in held], dtype=jnp.int32)
    device_ids = (my_row ^ row_masks) * cols + (my_col ^ col_masks)
    entries = device_ids[:, None] * held_tiles + jnp.arange(held_tiles, dtype=jnp.int32)
    entries = entries.reshape(-1)
    places = integral_list.reshape(-1)
    live = live_tiles.reshape(-1)

    matches = to_col[None, :] == (my_col ^ peers)[:, None]
    first, _ = nth(matches, 0)
    second, twice = nth(matches, 1)
    spare = jnp.logical_and(twice, peers > 0)
    extra = jnp.max(jnp.where(spare, second, 0))
    source = jnp.concatenate([first, second[:1], extra[None]])
    run = functools.partial(contract, pair_rows=pair_rows, inner_tiles=inner_tiles)
    outs = run(places, entries, live, source, amplitudes, mine, other, count=cols + 2)

    high = [1 << b for b in reversed(range(1, cols.bit_length() - 1))]
    carried = {0: outs[cols + 1]}
    for bit in high:
        for m in list(carried):
            if m == 0 or m in carried:
                carried[m | bit] = swap(carried[m], (0, bit), sizes)
    direct = {}
    for m in sorted(range(1, cols), key=lambda m: -(m & ~1)):
        direct[m] = swap(outs[m], (0, m), sizes)

    index = {m: n for n, m in enumerate(held)}
    lines = [index[(r, c)] for r in range(rows) for c in range(cols)]
    half = len(held) // 2

    def info(array):
        return array.reshape(half, held_tiles, META + width, width)[:, 0, width : width + 2, :tile_count]

    told = jnp.concatenate([info(mine), info(other)], axis=0).astype(jnp.int32)
    told = told[jnp.array(lines)].reshape(rows, cols, 2, tile_count)
    their_col, their_place = told[:, :, 0], told[:, :, 1]
    owners = (my_col ^ peers)[None, :, None]
    counts = jnp.sum((their_col[..., None] == peers).astype(jnp.int32), axis=2)
    spares = jnp.where(owners == peers, 0, jnp.maximum(counts - 1, 0))
    crowded = jnp.logical_or(
        jnp.any(jnp.sum(spares, axis=2) > 1), jnp.any(jnp.sum(spares, axis=1) > 1)
    )

    group_col, group_place = their_col[0], their_place[0]

    def landing(column, n):
        at, found = nth(group_col == column, n)
        spot = jnp.sum(jnp.where(jnp.arange(tile_count) == at[:, None], group_place, 0), axis=1)
        return jnp.where(found, spot, -1)

    firsts = landing(my_col, 0)
    seconds = landing(my_col, 1)
    onward = landing(my_col ^ 1, 1)
    evens = list(range(0, cols, 2))
    last = carried[0]
    for m in evens[1:]:
        last = jnp.where(onward[m] >= 0, carried[m], last)
    last = swap(last, (0, 1), sizes)
    odd = jnp.max(jnp.where(peers % 2 == 1, seconds, -1))

    base = [outs[0]] + [direct[m] for m in range(1, cols)] + [outs[cols]]
    even_arrivals = [carried[m] for m in evens[1:]]

    def balanced():
        positions = jnp.concatenate([firsts, seconds[jnp.array(evens)], odd[None]])
        return place(positions, base + even_arrivals + [last], tile_count)

    def crowded_exchange():
        slots = run(places, entries, live, second, amplitudes, mine, other, count=cols)
        slots = [slots[0]] + [swap(slots[m], (0, m), sizes) for m in range(1, cols)]
        positions = jnp.concatenate([firsts, seconds[:1], seconds[1:]])
        return place(positions, base + slots[1:], tile_count)

    return lax.cond(crowded, crowded_exchange, balanced)


def solution(mesh):
    in_specs = (
        P(("row", "col"), None),
        P(("row", "col"), None),
        P(("row", "col")),
        P(),
        P(("row", "col"), None, None),
    )
    out_specs = P(("row", "col"), None)
    body = functools.partial(shards, (mesh.shape["row"], mesh.shape["col"]))
    return jax.shard_map(body, mesh=mesh, in_specs=in_specs, out_specs=out_specs, check_vma=False)
```

```python
import functools

import jax
import jax.numpy as jnp
from jax import lax
from jax.experimental import pallas as pl
from jax.experimental.pallas import tpu as pltpu
from jax.sharding import PartitionSpec as P


AT = 8
META = 16


VMEM = pl.BlockSpec(memory_space=pltpu.VMEM)
SMEM = pl.BlockSpec(memory_space=pltpu.SMEM)
ANY = pl.BlockSpec(memory_space=pl.ANY)
HBM = pl.BlockSpec(memory_space=pltpu.HBM)
NONE = 1 << 20


def swap(value, mask, sizes):
    rows, cols = sizes
    pairs = [
        (r * cols + c, (r ^ mask[0]) * cols + (c ^ mask[1]))
        for r in range(rows)
        for c in range(cols)
    ]
    return lax.ppermute(value, ("row", "col"), pairs)


def gather_all(block, tables, sizes):
    rows, cols = sizes
    step = cols // 4
    far = [(0, m * step) for m in range(4)]
    near = [(2 * i, j) for i in range(rows // 2) for j in range(step)]
    pieces = {0: block}
    for m in (3, 2, 1):
        pieces[m] = swap(block, far[m], sizes)
    line = jnp.concatenate([pieces[m] for m in range(4)], axis=0)
    line, tables = lax.optimization_barrier((line, tables))
    parts = [line]
    order = list(reversed(near[1:]))
    for mask in order:
        parts.append(swap(line, mask, sizes))
    mine = jnp.concatenate(parts, axis=0)
    other = swap(mine, (1, 0), sizes)
    return mine, other, tables


def gather_masks(sizes):
    rows, cols = sizes
    step = cols // 4
    far = [(0, m * step) for m in range(4)]
    near = [(2 * i, j) for i in range(rows // 2) for j in range(step)]
    masks = [near[0]] + list(reversed(near[1:]))
    held = [(a[0] ^ b[0], a[1] ^ b[1]) for a in masks for b in far]
    return held + [(a ^ 1, b) for a, b in held]


def contract_kernel(pair_rows, inner_tiles, unroll, source, tables, amp, mine, other, *rest):
    outs, total = rest[:-1], rest[-1]
    count = 2 * mine.shape[0]
    half = mine.shape[0]
    width = mine.shape[2]
    tiles = amp.shape[0] // pair_rows
    total[...] = jnp.zeros_like(total)

    def add_tiles(ref, base):
        def step(q, carry):
            k, a = tables[base + q], tables[count + base + q]
            inner = pl.ds(pl.multiple_of(k * width, width), width)
            outer = pl.ds(pl.multiple_of(a * width, width), width)
            parts = []
            for s in range(tiles):
                part = amp[s * pair_rows : (s + 1) * pair_rows, inner]
                alive = tables[2 * count + s * inner_tiles + k] != 0
                parts.append(jnp.where(alive, part, jnp.zeros_like(part)))
            left = jnp.concatenate(parts, axis=0)
            right = ref[q, pl.ds(0, width), :]
            total[:, outer] += jnp.dot(left, right, preferred_element_type=jnp.float32)
            return carry

        lax.fori_loop(0, half, step, 0, unroll=min(unroll, half))

    add_tiles(mine, 0)
    add_tiles(other, half)
    for n, out in enumerate(outs):
        start = pl.multiple_of(source[n] * pair_rows, pair_rows)
        out[...] = total[pl.ds(start, pair_rows), :].astype(out.dtype)


def contract(source, tables, amp, mine, other, count, pair_rows, inner_tiles):
    width = mine.shape[2]
    body = functools.partial(contract_kernel, pair_rows, inner_tiles, 16)
    return pl.pallas_call(
        body,
        out_shape=[jax.ShapeDtypeStruct((pair_rows, AT * width), amp.dtype)] * count,
        in_specs=[SMEM] * 2 + [VMEM] * 3,
        out_specs=[VMEM] * count,
        scratch_shapes=[pltpu.VMEM((amp.shape[0], AT * width), jnp.float32)],
        compiler_params=pltpu.CompilerParams(vmem_limit_bytes=40 * 1024 * 1024),
        name="contract",
    )(source, tables, amp, mine, other)


def destinations(block, width):
    told = block[pl.ds(width, META), :].astype(jnp.float32)
    return told[0:1], told[1:2]


def arrivals_kernel(slots, width, mine, positions, onward):
    my_col = lax.axis_index("col")
    told = [destinations(mine.at[q], width) for q in slots]
    column = jnp.concatenate([t[0] for t in told], axis=0).astype(jnp.int32)
    spot = jnp.concatenate([t[1] for t in told], axis=0).astype(jnp.int32)
    lane = lax.broadcasted_iota(jnp.int32, column.shape, 1)

    def landing(owner):
        match = column == owner
        first = jnp.min(jnp.where(match, lane, NONE), axis=1, keepdims=True)
        match = jnp.logical_and(match, lane != first)
        second = jnp.min(jnp.where(match, lane, NONE), axis=1, keepdims=True)

        def spot_at(at):
            found = jnp.sum(jnp.where(lane == at, spot, 0), axis=1, keepdims=True)
            return jnp.where(at < NONE, found, -1)

        return spot_at(first), spot_at(second)

    first, second = landing(my_col)
    _, passed = landing(my_col ^ 1)
    for m in range(len(slots)):
        positions[m] = first[m, 0]
        positions[len(slots) + m] = second[m, 0]
    chosen, odd = jnp.int32(0), jnp.int32(-1)
    for m in range(2, len(slots), 2):
        chosen = jnp.where(passed[m, 0] >= 0, m, chosen)
    for m in range(1, len(slots), 2):
        odd = jnp.maximum(odd, second[m, 0])
    onward[0] = chosen
    positions[2 * len(slots)] = odd


def arrivals(mine, slots, width):
    return pl.pallas_call(
        functools.partial(arrivals_kernel, slots, width),
        out_shape=[
            jax.ShapeDtypeStruct((2 * len(slots) + 1,), jnp.int32),
            jax.ShapeDtypeStruct((1,), jnp.int32),
        ],
        in_specs=[VMEM],
        out_specs=[SMEM, SMEM],
        name="arrivals",
    )(mine)


def crowding_kernel(groups, width, mine, other, crowded):
    my_col = lax.axis_index("col")
    half = mine.shape[0]
    worst = jnp.int32(0)
    for slots in groups:
        blocks = [(mine.at[q] if q < half else other.at[q - half]) for q in slots]
        column = jnp.concatenate([destinations(b, width)[0] for b in blocks], axis=0)
        column = column.astype(jnp.int32)
        lane = lax.broadcasted_iota(jnp.int32, column.shape, 1)
        owner = lax.broadcasted_iota(jnp.int32, column.shape, 0) ^ my_col
        spare = jnp.zeros(column.shape, jnp.int32)
        for d in range(len(slots)):
            count = jnp.sum((column == d).astype(jnp.int32), axis=1, keepdims=True)
            spare = jnp.where(lane == d, jnp.maximum(count - 1, 0), spare)
        spare = jnp.where(lane == owner, 0, spare)
        sent = jnp.max(jnp.sum(spare, axis=1, keepdims=True))
        taken = jnp.max(jnp.sum(spare, axis=0, keepdims=True))
        worst = jnp.maximum(worst, jnp.maximum(sent, taken))
    crowded[0] = worst


def crowding(mine, other, groups, width):
    return pl.pallas_call(
        functools.partial(crowding_kernel, groups, width),
        out_shape=jax.ShapeDtypeStruct((1,), jnp.int32),
        in_specs=[VMEM, VMEM],
        out_specs=SMEM,
        name="crowding",
    )(mine, other)


def choose_kernel(onward, *rest):
    choices, out, sem = rest[:-2], rest[-2], rest[-1]
    for n, choice in enumerate(choices):

        @pl.when(onward[0] == 2 * n)
        def _(choice=choice):
            copy = pltpu.make_async_copy(choice, out, sem)
            copy.start()
            copy.wait()


def choose(onward, choices):
    return pl.pallas_call(
        choose_kernel,
        out_shape=jax.ShapeDtypeStruct(choices[0].shape, choices[0].dtype),
        in_specs=[SMEM] + [ANY] * len(choices),
        out_specs=VMEM,
        scratch_shapes=[pltpu.SemaphoreType.DMA],
        name="choose",
    )(onward, *choices)


def place_kernel(places, positions, *rest):
    sources = rest[: len(places)]
    out, left = rest[-2:]
    rows = sources[0].shape[0]

    def store(n, source):
        start = pl.multiple_of(jnp.maximum(positions[places[n]], 0) * rows, rows)
        return pltpu.make_async_copy(source, out.at[pl.ds(start, rows), :], left.at[n])

    for n, source in enumerate(sources):
        pl.when(positions[places[n]] >= 0)(lambda n=n, source=source: store(n, source).start())
    for n, source in enumerate(sources):
        pl.when(positions[places[n]] >= 0)(lambda n=n, source=source: store(n, source).wait())


def place(places, positions, sources, tile_count, ladder=None):
    rows, width = sources[0].shape
    count = len(sources)
    into = [] if ladder is None else [ladder]
    return pl.pallas_call(
        functools.partial(place_kernel, places),
        out_shape=pltpu.HBM((tile_count * rows, width), sources[0].dtype),
        in_specs=[SMEM] + [VMEM] * count + [HBM] * len(into),
        out_specs=HBM,
        scratch_shapes=[pltpu.SemaphoreType.DMA((count,))],
        input_output_aliases={1 + count: 0} if into else {},
        name="place",
    )(positions, *sources, *into)


def nth(matches, n):
    size = matches.shape[-1]
    index = jnp.arange(size, dtype=jnp.int32)
    earlier = index[None, :] < index[:, None]
    rank = jnp.sum(jnp.logical_and(matches[..., None, :], earlier), axis=-1)
    chosen = jnp.logical_and(matches, rank == n)
    return jnp.sum(jnp.where(chosen, index, 0), axis=-1), jnp.any(chosen, axis=-1)


def shards(sizes, *arrays):
    return step(sizes, *arrays)


def hops(cols):
    high = [1 << b for b in reversed(range(1, cols.bit_length() - 1))]
    far = [(None, m) for m in reversed(range(high[0], cols))]
    near = [(None, m) for m in reversed(range(1, high[0]))]
    late, known = [], [0]
    for bit in high:
        late += [(m, bit) for m in known if m]
        known += [m | bit for m in known]
    early = [(0, bit) for bit in high] + near + far[:1]
    return early + late + far[1:]


def step(sizes, amplitudes, live_tiles, destination, integral_list, integral_tiles):
    rows, cols = sizes
    tile_count = destination.shape[0]
    pair_rows = amplitudes.shape[0] // tile_count
    inner_tiles = live_tiles.shape[1]
    held_tiles, width, _ = integral_tiles.shape
    my_row, my_col = lax.axis_index("row"), lax.axis_index("col")
    peers = jnp.arange(cols, dtype=jnp.int32)
    held = gather_masks(sizes)

    to_col = destination // tile_count % cols
    to_place = destination % tile_count
    meta = jnp.stack([to_col, to_place]).astype(integral_tiles.dtype)
    meta = jnp.pad(meta, ((0, META - 2), (0, width - tile_count)), constant_values=-1)
    meta = jnp.broadcast_to(meta[None], (held_tiles, META, width))
    block = jnp.concatenate([integral_tiles, meta], axis=1)

    matches = to_col[None, :] == (my_col ^ peers)[:, None]
    first, _ = nth(matches, 0)
    second, twice = nth(matches, 1)
    spare = jnp.logical_and(twice, peers > 0)
    extra = jnp.max(jnp.where(spare, second, 0))
    source = jnp.concatenate([first, second[:1], extra[None]])

    row_masks = jnp.array([m[0] for m in held], dtype=jnp.int32)
    col_masks = jnp.array([m[1] for m in held], dtype=jnp.int32)
    device_ids = (my_row ^ row_masks) * cols + (my_col ^ col_masks)
    entries = device_ids[:, None] * held_tiles + jnp.arange(held_tiles, dtype=jnp.int32)
    picked = integral_list[entries.reshape(-1)]
    tables = jnp.concatenate([picked[:, 0], picked[:, 1], live_tiles.reshape(-1)])

    mine, other, (source, tables) = gather_all(block, (source, tables), sizes)
    run = functools.partial(contract, pair_rows=pair_rows, inner_tiles=inner_tiles)
    outs = run(source, tables, amplitudes, mine, other, count=cols + 2)

    carried, direct = {0: outs[cols + 1]}, {}
    for hop in hops(cols):
        m, bit = hop
        if m is None:
            direct[bit] = swap(outs[bit], (0, bit), sizes)
        else:
            carried[m | bit] = swap(carried[m], (0, bit), sizes)

    index = {m: n * held_tiles for n, m in enumerate(held)}
    groups = [[index[(r, c)] for c in range(cols)] for r in range(rows)]
    positions, onward = arrivals(mine, groups[0], width)
    crowded = crowding(mine, other, groups, width)

    evens = list(range(2, cols, 2))
    last = choose(onward, [carried[0]] + [carried[m] for m in evens])
    last = swap(last, (0, 1), sizes)

    base = [outs[0]] + [direct[m] for m in range(1, cols)] + [outs[cols]]
    ladder = place(list(range(cols + 1)), positions, base, tile_count)
    spots = [cols + m for m in evens] + [2 * cols]
    ladder = place(spots, positions, [carried[m] for m in evens] + [last], tile_count, ladder)

    def again(state):
        return state[0] > 1

    def send_seconds(state):
        slots = run(second, tables, amplitudes, mine, other, count=cols)
        slots = [swap(slots[m], (0, m), sizes) for m in range(1, cols)]
        spots = list(range(cols + 1, 2 * cols))
        return jnp.zeros_like(state[0]), place(spots, positions, slots, tile_count, state[1])

    return lax.while_loop(again, send_seconds, (crowded[0], ladder))[1]


def solution(mesh):
    in_specs = (
        P(("row", "col"), None),
        P(("row", "col"), None),
        P(("row", "col")),
        P(),
        P(("row", "col"), None, None),
    )
    out_specs = P(("row", "col"), None)
    body = functools.partial(shards, (mesh.shape["row"], mesh.shape["col"]))
    return jax.shard_map(body, mesh=mesh, in_specs=in_specs, out_specs=out_specs, check_vma=False)
```

```python
import functools

import jax
import jax.numpy as jnp
from jax import lax
from jax.experimental import pallas as pl
from jax.experimental.pallas import tpu as pltpu
from jax.sharding import PartitionSpec as P


AT = 8
META = 16


GRANT = pltpu.CompilerParams(vmem_limit_bytes=40 * 1024 * 1024)
SMALL = pltpu.CompilerParams(vmem_limit_bytes=12 * 1024 * 1024)
VMEM = pl.BlockSpec(memory_space=pltpu.VMEM)
SMEM = pl.BlockSpec(memory_space=pltpu.SMEM)
ANY = pl.BlockSpec(memory_space=pl.ANY)
HBM = pl.BlockSpec(memory_space=pltpu.HBM)
NONE = 1 << 20
LAST = (None, None)


def swap(value, mask, sizes):
    rows, cols = sizes
    pairs = [
        (r * cols + c, (r ^ mask[0]) * cols + (c ^ mask[1]))
        for r in range(rows)
        for c in range(cols)
    ]
    return lax.ppermute(value, ("row", "col"), pairs)


def local(value):
    return pltpu.with_memory_space_constraint(value, pltpu.VMEM)


def join_kernel(*refs):
    out = refs[-1]
    size = refs[0].shape[0]
    for n, ref in enumerate(refs[:-1]):
        out[n * size : (n + 1) * size] = ref[...]


def join(pieces):
    shape = pieces[0].shape
    return pl.pallas_call(
        join_kernel,
        out_shape=pltpu.VMEM((len(pieces) * shape[0], *shape[1:]), pieces[0].dtype),
        in_specs=[VMEM] * len(pieces),
        out_specs=VMEM,
        compiler_params=SMALL,
        name="join",
    )(*[local(piece) for piece in pieces])


def gather_all(block, sizes):
    rows, cols = sizes
    step = cols // 4
    near = [(2 * i, j) for i in range(rows // 2) for j in range(step)]
    pieces = {0: block}
    for m in (3, 2, 1):
        pieces[m] = swap(block, (0, m * step), sizes)
    line = join([pieces[m] for m in range(4)])
    mine, other = {0: line}, {}
    for n in reversed(range(1, len(near))):
        mine[n] = swap(line, near[n], sizes)
    for n in range(len(near)):
        other[n] = swap(mine[n], (1, 0), sizes)
    count = range(len(near))
    return [local(mine[n]) for n in count], [local(other[n]) for n in count]


def gather_mask(q, half, cols):
    step = cols // 4
    line, far = divmod(q, 4)
    return 2 * (line // step) + half, line % step + far * step


def mask_kernel(pair_rows, width, live, amp, out, sems):
    tiles = amp.shape[0] // pair_rows

    def fetch(s):
        rows = pl.ds(s * pair_rows, pair_rows)
        return pltpu.make_async_copy(amp.at[rows, :], out.at[rows, :], sems.at[s])

    for s in range(tiles):
        fetch(s).start()
    for s in range(tiles):
        fetch(s).wait()
        for k in range(amp.shape[1] // width):
            part = out[s * pair_rows : (s + 1) * pair_rows, k * width : (k + 1) * width]
            part = jnp.where(live[s, k] != 0, part, jnp.zeros_like(part))
            out[s * pair_rows : (s + 1) * pair_rows, k * width : (k + 1) * width] = part


def mask_amplitudes(live, amp, pair_rows, width):
    tiles = amp.shape[0] // pair_rows
    return pl.pallas_call(
        functools.partial(mask_kernel, pair_rows, width),
        out_shape=pltpu.VMEM(amp.shape, amp.dtype),
        in_specs=[SMEM, HBM],
        out_specs=VMEM,
        scratch_shapes=[pltpu.SemaphoreType.DMA((tiles,))],
        compiler_params=SMALL,
        name="mask",
    )(live, pltpu.with_memory_space_constraint(amp, pltpu.HBM))


def add_tiles(places, total, refs, half, held_tiles, cols, rows):
    my_row, my_col = lax.axis_index("row"), lax.axis_index("col")
    base, step = places_at(cols), cols // 4

    def add(ref, line, q):
        width = ref.shape[2]
        far = q // held_tiles
        row_mask, col_mask = 2 * (line // step) + half, line % step + far * step
        entry = ((my_row ^ row_mask) * cols + (my_col ^ col_mask)) * held_tiles + q % held_tiles
        k, a = places[base + 2 * entry], places[base + 2 * entry + 1]
        inner = pl.ds(pl.multiple_of(k * width, width), width)
        outer = pl.ds(pl.multiple_of(a * width, width), width)
        right = ref[q, pl.ds(0, width), :]
        total[:, outer] += jnp.dot(rows(inner), right, preferred_element_type=jnp.float32)

    for line, ref in enumerate(refs):
        for q in range(ref.shape[0]):
            add(ref, line, q)


def contract_mine_kernel(held_tiles, cols, table, amp, *rest):
    mine, total = rest[:-1], rest[-1]
    total[...] = jnp.zeros_like(total)
    add_tiles(table, total, mine, 0, held_tiles, cols, lambda inner: amp[:, inner])


def contract_one_kernel(slot, pair_rows, held_tiles, cols, table, amp, given, *rest):
    other, (out, _, one) = rest[:-3], rest[-3:]
    picked = pl.ds(pl.multiple_of(table[slot] * pair_rows, pair_rows), pair_rows)
    one[...] = given[picked, :]
    add_tiles(table, one, other, 1, held_tiles, cols, lambda inner: amp[picked, inner])
    out[...] = one[...].astype(out.dtype)


def contract_rest_kernel(slots, own, parts, pair_rows, held_tiles, cols, table, amp, given, *rest):
    other, rest = rest[:parts], rest[parts:]
    outs = rest[: len(slots)]
    if own:
        total, ladder, kept, sems = rest[len(slots) :]
    else:
        (total,) = rest[len(slots) :]
    add_tiles(table, total, other, 1, held_tiles, cols, lambda inner: amp[:, inner])

    def product(slot):
        start = pl.multiple_of(table[slot] * pair_rows, pair_rows)
        return total[pl.ds(start, pair_rows), :]

    copies = []
    for n, (slot, where) in enumerate(own):
        start = pl.multiple_of(jnp.maximum(table[where], 0) * pair_rows, pair_rows)
        kept[n] = product(slot).astype(kept.dtype)
        copy = pltpu.make_async_copy(kept.at[n], ladder.at[pl.ds(start, pair_rows), :], sems.at[n])
        copies.append((table[where] >= 0, copy))
        pl.when(table[where] >= 0)(copy.start)
    for slot, out in zip(slots, outs):
        out[...] = product(slot).astype(out.dtype)
    for there, copy in copies:
        pl.when(there)(copy.wait)


def contract_mine(table, amp, mine, sizes):
    return pl.pallas_call(
        functools.partial(contract_mine_kernel, *sizes[1:]),
        out_shape=pltpu.VMEM((amp.shape[0], AT * mine[0].shape[2]), jnp.float32),
        in_specs=[SMEM, VMEM] + [VMEM] * len(mine),
        out_specs=VMEM,
        compiler_params=GRANT,
        name="contract_mine",
    )(table, amp, *mine)


def contract_one(slot, table, amp, other, total, sizes):
    shape = (sizes[0], total.shape[1])
    return pl.pallas_call(
        functools.partial(contract_one_kernel, slot, *sizes),
        out_shape=[pltpu.VMEM(shape, amp.dtype), pltpu.VMEM(total.shape, total.dtype)],
        in_specs=[SMEM, VMEM, VMEM] + [VMEM] * len(other),
        out_specs=[VMEM, VMEM],
        scratch_shapes=[pltpu.VMEM(shape, jnp.float32)],
        input_output_aliases={2: 1},
        compiler_params=GRANT,
        name="contract_one",
    )(table, amp, total, *other)


def contract_rest(slots, own, table, amp, other, total, sizes):
    shape = (sizes[0], total.shape[1])
    out_shape = [pltpu.VMEM(shape, amp.dtype)] * len(slots)
    out_shape.append(pltpu.VMEM(total.shape, total.dtype))
    scratch = []
    if own:
        out_shape.append(pltpu.HBM(total.shape, amp.dtype))
        scratch = [pltpu.VMEM((len(own), *shape), amp.dtype), pltpu.SemaphoreType.DMA((len(own),))]
    return pl.pallas_call(
        functools.partial(contract_rest_kernel, slots, own, len(other), *sizes),
        out_shape=out_shape,
        in_specs=[SMEM, VMEM, VMEM] + [VMEM] * len(other),
        out_specs=[VMEM] * (len(slots) + 1) + [HBM] * (1 if own else 0),
        scratch_shapes=scratch,
        input_output_aliases={2: len(slots)},
        compiler_params=GRANT,
        name="contract_rest",
    )(table, amp, total, *other)


def places_at(cols):
    return 3 * cols + 4


def table_kernel(cols, destination, integrals, table):
    my_col = lax.axis_index("col")
    count = destination.shape[0]
    again, seen_at, base = cols + 4, 2 * cols + 4, places_at(cols)
    for n in range(base):
        table[n] = 0
    table[cols + 2] = -1
    table[cols + 3] = -1
    for s in range(count):
        mask = destination[s] // count % cols ^ my_col
        spot = destination[s] % count
        seen = table[seen_at + mask]
        table[seen_at + mask] = seen + 1

        @pl.when(seen == 0)
        def _(s=s, mask=mask):
            table[mask] = s

        @pl.when(seen > 0)
        def _(s=s, mask=mask):
            table[again + mask] = s

        @pl.when(mask == 0)
        def _(s=s, seen=seen, spot=spot):
            table[cols + 2 + jnp.minimum(seen, 1)] = spot

        @pl.when(jnp.logical_and(mask == 0, seen > 0))
        def _(s=s):
            table[cols] = s

        @pl.when(jnp.logical_and(mask != 0, seen > 0))
        def _(s=s):
            table[cols + 1] = s

    for n in range(integrals.shape[0]):
        table[base + 2 * n] = integrals[n, 0]
        table[base + 2 * n + 1] = integrals[n, 1]


def make_table(destination, integrals, cols):
    size = places_at(cols) + 2 * integrals.shape[0]
    return pl.pallas_call(
        functools.partial(table_kernel, cols),
        out_shape=pltpu.SMEM((size,), jnp.int32),
        in_specs=[SMEM, SMEM],
        out_specs=SMEM,
        compiler_params=SMALL,
        name="table",
    )(destination, integrals)


def destinations(block, width):
    told = block[pl.ds(width, META), :].astype(jnp.float32)
    return told[0:1], told[1:2]


def arrivals_kernel(slots, width, *refs):
    my_col = lax.axis_index("col")
    mine, (positions, onward) = refs[:-2], refs[-2:]
    told = [destinations(mine[n].at[q], width) for n, q in slots]
    column = jnp.concatenate([t[0] for t in told], axis=0).astype(jnp.int32)
    spot = jnp.concatenate([t[1] for t in told], axis=0).astype(jnp.int32)
    lane = lax.broadcasted_iota(jnp.int32, column.shape, 1)

    def landing(owner):
        match = column == owner
        first = jnp.min(jnp.where(match, lane, NONE), axis=1, keepdims=True)
        match = jnp.logical_and(match, lane != first)
        second = jnp.min(jnp.where(match, lane, NONE), axis=1, keepdims=True)

        def spot_at(at):
            found = jnp.sum(jnp.where(lane == at, spot, 0), axis=1, keepdims=True)
            return jnp.where(at < NONE, found, -1)

        return spot_at(first), spot_at(second)

    first, second = landing(my_col)
    _, passed = landing(my_col ^ 1)
    for m in range(len(slots)):
        positions[m] = first[m, 0]
        positions[len(slots) + m] = second[m, 0]
    chosen, odd = jnp.int32(0), jnp.int32(-1)
    for m in range(2, len(slots), 2):
        chosen = jnp.where(passed[m, 0] >= 0, m, chosen)
    for m in range(1, len(slots), 2):
        odd = jnp.maximum(odd, second[m, 0])
    onward[0] = chosen
    positions[2 * len(slots)] = odd


def arrivals(mine, slots, width):
    return pl.pallas_call(
        functools.partial(arrivals_kernel, slots, width),
        out_shape=[
            pltpu.SMEM((2 * len(slots) + 1,), jnp.int32),
            pltpu.SMEM((1,), jnp.int32),
        ],
        in_specs=[VMEM] * len(mine),
        out_specs=[SMEM, SMEM],
        compiler_params=SMALL,
        name="arrivals",
    )(*mine)


def crowding_kernel(groups, width, *refs):
    my_col = lax.axis_index("col")
    refs, crowded = refs[:-1], refs[-1]
    worst = jnp.int32(0)
    for slots in groups:
        blocks = [refs[n].at[q] for n, q in slots]
        column = jnp.concatenate([destinations(b, width)[0] for b in blocks], axis=0)
        column = column.astype(jnp.int32)
        lane = lax.broadcasted_iota(jnp.int32, column.shape, 1)
        owner = lax.broadcasted_iota(jnp.int32, column.shape, 0) ^ my_col
        spare = jnp.zeros(column.shape, jnp.int32)
        for d in range(len(slots)):
            count = jnp.sum((column == d).astype(jnp.int32), axis=1, keepdims=True)
            spare = jnp.where(lane == d, jnp.maximum(count - 1, 0), spare)
        spare = jnp.where(lane == owner, 0, spare)
        sent = jnp.max(jnp.sum(spare, axis=1, keepdims=True))
        taken = jnp.max(jnp.sum(spare, axis=0, keepdims=True))
        worst = jnp.maximum(worst, jnp.maximum(sent, taken))
    crowded[0] = worst


def crowding(blocks, groups, width):
    return pl.pallas_call(
        functools.partial(crowding_kernel, groups, width),
        out_shape=jax.ShapeDtypeStruct((1,), jnp.int32),
        in_specs=[VMEM] * len(blocks),
        out_specs=SMEM,
        compiler_params=SMALL,
        name="crowding",
    )(*blocks)


def choose_kernel(onward, *rest):
    choices, out = rest[:-1], rest[-1]
    for n, choice in enumerate(choices):

        @pl.when(onward[0] == 2 * n)
        def _(choice=choice):
            out[...] = choice[...]


def choose(onward, choices):
    return pl.pallas_call(
        choose_kernel,
        out_shape=pltpu.VMEM(choices[0].shape, choices[0].dtype),
        in_specs=[SMEM] + [VMEM] * len(choices),
        out_specs=VMEM,
        compiler_params=SMALL,
        name="choose",
    )(onward, *choices)


def place_kernel(places, guarded, crowded, positions, *rest):
    sources = rest[: len(places)]
    out, left = rest[-2:]
    rows = sources[0].shape[0]

    def there(n):
        here = positions[places[n]] >= 0
        return jnp.logical_and(here, crowded[0] <= 1) if places[n] == guarded else here

    def store(n):
        start = pl.multiple_of(jnp.maximum(positions[places[n]], 0) * rows, rows)
        return pltpu.make_async_copy(sources[n], out.at[pl.ds(start, rows), :], left.at[n])

    for n in range(len(places)):
        pl.when(there(n))(lambda n=n: store(n).start())
    for n in range(len(places)):
        pl.when(there(n))(lambda n=n: store(n).wait())


def place(places, crowded, positions, sources, ladder, guarded=None):
    count = len(sources)
    return pl.pallas_call(
        functools.partial(place_kernel, places, guarded),
        out_shape=pltpu.HBM(ladder.shape, ladder.dtype),
        in_specs=[SMEM, SMEM] + [VMEM] * count + [HBM],
        out_specs=HBM,
        scratch_shapes=[pltpu.SemaphoreType.DMA((count,))],
        input_output_aliases={2 + count: 0},
        compiler_params=SMALL,
        name="place",
    )(crowded, positions, *sources, ladder)


def shards(sizes, *arrays):
    return step(sizes, *arrays)


def make_block(destination, integral_tiles, cols):
    tile_count = destination.shape[0]
    held_tiles, width, _ = integral_tiles.shape
    to_col = destination // tile_count % cols
    to_place = destination % tile_count
    meta = jnp.stack([to_col, to_place]).astype(integral_tiles.dtype)
    meta = jnp.pad(meta, ((0, META - 2), (0, width - tile_count)), constant_values=-1)
    meta = jnp.broadcast_to(meta[None], (held_tiles, META, width))
    return jnp.concatenate([integral_tiles, meta], axis=1)


def hops(cols):
    high = [1 << b for b in reversed(range(1, cols.bit_length() - 1))]
    far = [(None, m) for m in reversed(range(high[0], cols))]
    near = [(None, m) for m in reversed(range(1, high[0]))]
    late, known = [], [0]
    for bit in high:
        late += [(m, bit) for m in known if m]
        known += [m | bit for m in known]
    order = [(0, bit) for bit in high] + far[:1] + near[-1:] + late
    rest = []
    for n, hop in enumerate(far[1:]):
        rest += [hop] + near[:-1][n : n + 1]
    return order + rest[:-1] + [LAST] + rest[-1:]


def step(sizes, amplitudes, live_tiles, destination, integral_list, integral_tiles):
    rows, cols = sizes
    tile_count = destination.shape[0]
    pair_rows = amplitudes.shape[0] // tile_count
    held_tiles, width, _ = integral_tiles.shape
    block = make_block(destination, integral_tiles, cols)
    masked = mask_amplitudes(live_tiles, amplitudes, pair_rows, width)
    mine, other = gather_all(block, sizes)
    table = make_table(destination, integral_list, cols)
    shape = (pair_rows, held_tiles, cols)
    total = contract_mine(table, masked, mine, shape)
    extra_tile, total = contract_one(cols + 1, table, masked, other, total, shape)
    slots = list(range(1, cols))
    own = [(0, cols + 2), (cols, cols + 3)]
    *outs, _, ladder = contract_rest(slots, own, table, masked, other, total, shape)

    held = [gather_mask(q, half, cols) for half in (0, 1) for q in range(rows * cols // 2)]
    index = {m: (n // 4, n % 4 * held_tiles) for n, m in enumerate(held)}
    groups = [[index[(r, c)] for c in range(cols)] for r in range(rows)]
    positions, onward = arrivals(mine, groups[0], width)
    crowded = crowding(mine + other, groups, width)

    evens = list(range(2, cols, 2))
    carried, direct = {0: extra_tile}, {}
    for hop in hops(cols):
        m, bit = hop
        if hop == LAST:
            last = choose(onward, [carried[0]] + [carried[m] for m in evens])
            last = local(swap(last, (0, 1), sizes))
        elif m is None:
            direct[bit] = local(swap(outs[bit - 1], (0, bit), sizes))
        else:
            carried[m | bit] = local(swap(carried[m], (0, bit), sizes))

    soon, late = list(range(1, cols // 2)), list(range(cols // 2, cols))
    soon, late = soon + late[-2:], late[:-2]
    spots = soon + [cols + m for m in evens]
    sources = [direct[m] for m in soon] + [carried[m] for m in evens]
    ladder = place(spots, crowded, positions, sources, ladder)

    def again(state):
        return state[0] > 1

    def send_seconds(state):
        mine, other = gather_all(make_block(destination, integral_tiles, cols), sizes)
        table = make_table(destination, integral_list, cols)
        masked = mask_amplitudes(live_tiles, amplitudes, pair_rows, width)
        total = contract_mine(table, masked, mine, shape)
        again = [cols + 4 + m for m in slots]
        *outs, _ = contract_rest(again, [], table, masked, other, total, shape)
        outs = [local(swap(out, (0, m), sizes)) for m, out in zip(slots, outs)]
        spots = list(range(cols + 1, 2 * cols))
        return jnp.zeros_like(state[0]), place(spots, crowded, positions, outs, state[1])

    ladder = lax.while_loop(again, send_seconds, (crowded[0], ladder))[1]

    sources = [direct[m] for m in late] + [last]
    return place(late + [2 * cols], crowded, positions, sources, ladder, 2 * cols)


def solution(mesh):
    in_specs = (
        P(("row", "col"), None),
        P(("row", "col"), None),
        P(("row", "col")),
        P(),
        P(("row", "col"), None, None),
    )
    out_specs = P(("row", "col"), None)
    body = functools.partial(shards, (mesh.shape["row"], mesh.shape["col"]))
    return jax.shard_map(body, mesh=mesh, in_specs=in_specs, out_specs=out_specs, check_vma=False)
```

```python
import functools

import jax
import jax.numpy as jnp
from jax import lax
from jax.experimental import pallas as pl
from jax.experimental.pallas import tpu as pltpu
from jax.sharding import PartitionSpec as P


AT = 8


GRANT = pltpu.CompilerParams(vmem_limit_bytes=40 * 1024 * 1024)
SMALL = pltpu.CompilerParams(vmem_limit_bytes=12 * 1024 * 1024)
VMEM = pl.BlockSpec(memory_space=pltpu.VMEM)
SMEM = pl.BlockSpec(memory_space=pltpu.SMEM)
ANY = pl.BlockSpec(memory_space=pl.ANY)
HBM = pl.BlockSpec(memory_space=pltpu.HBM)
LAST = (None, None)
NONE = 1 << 20
META = 16


def swap(value, mask, sizes):
    rows, cols = sizes
    pairs = [
        (r * cols + c, (r ^ mask[0]) * cols + (c ^ mask[1]))
        for r in range(rows)
        for c in range(cols)
    ]
    return lax.ppermute(value, ("row", "col"), pairs)


def local(value):
    return pltpu.with_memory_space_constraint(value, pltpu.VMEM)


def block_kernel(cols, destination, integrals, out, rows):
    held, width, _ = integrals.shape
    tiles = destination.shape[1]
    rows[...] = jnp.full(rows.shape, -1.0, rows.dtype)
    owner, spot = split(destination[...], tiles)
    rows[0:1, :tiles] = split(owner, cols)[1].astype(rows.dtype)
    rows[1:2, :tiles] = spot.astype(rows.dtype)
    for t in range(held):
        out[t, :width, :] = integrals[t]
        out[t, width:, :] = rows[...].astype(out.dtype)


def make_block(destination, integrals, cols):
    held, width, _ = integrals.shape
    return pl.pallas_call(
        functools.partial(block_kernel, cols),
        out_shape=pltpu.VMEM((held, width + META, width), integrals.dtype),
        in_specs=[VMEM, VMEM],
        out_specs=VMEM,
        scratch_shapes=[pltpu.VMEM((META, width), jnp.float32)],
        compiler_params=SMALL,
        name="block",
    )(destination[None], integrals)


def join_kernel(*refs):
    pieces, out, rows = refs[:4], refs[4], refs[5]
    held, _, width = pieces[0].shape
    rows[...] = jnp.full(rows.shape, -1.0, rows.dtype)
    for n, piece in enumerate(pieces):
        for t in range(held):
            start = (n * held + t) * width
            out[start : start + width, :] = piece[t, :width, :]
        told = piece[0, width:, :].astype(rows.dtype)
        rows[2 * n : 2 * n + 2, :] = told[0:2]
    out[4 * held * width :, :] = rows[...].astype(out.dtype)


def join(pieces):
    held, _, width = pieces[0].shape
    return pl.pallas_call(
        join_kernel,
        out_shape=pltpu.VMEM((4 * held * width + META, width), pieces[0].dtype),
        in_specs=[VMEM] * 4,
        out_specs=VMEM,
        scratch_shapes=[pltpu.VMEM((META, width), jnp.float32)],
        compiler_params=SMALL,
        name="join",
    )(*[local(x) for x in pieces])


def gather_all(block, sizes):
    rows, cols = sizes
    step = cols // 4
    near = [(2 * i, j) for i in range(rows // 2) for j in range(step)]
    pieces = {0: block}
    for m in (3, 2, 1):
        pieces[m] = swap(block, (0, m * step), sizes)
    line = join([pieces[m] for m in range(4)])
    mine, other = {0: line}, {}
    for n in reversed(range(1, len(near))):
        mine[n] = swap(line, near[n], sizes)
    for n in mine:
        other[n] = swap(mine[n], (1, 0), sizes)
    gathered = {(0, n): local(mine[n]) for n in mine}
    gathered.update({(1, n): local(other[n]) for n in other})
    return gathered, list(mine)


def gather_mask(q, half, cols):
    step = cols // 4
    line, far = divmod(q, 4)
    return 2 * (line // step) + half, line % step + far * step


def mask_kernel(pair_rows, width, live, amp, out, sems):
    tiles = amp.shape[0] // pair_rows

    def fetch(s):
        rows = pl.ds(s * pair_rows, pair_rows)
        return pltpu.make_async_copy(amp.at[rows, :], out.at[rows, :], sems.at[s])

    for s in range(tiles):
        fetch(s).start()
    for s in range(tiles):
        fetch(s).wait()
        for k in range(amp.shape[1] // width):
            part = out[s * pair_rows : (s + 1) * pair_rows, k * width : (k + 1) * width]
            part = jnp.where(live[s, k] != 0, part, jnp.zeros_like(part))
            out[s * pair_rows : (s + 1) * pair_rows, k * width : (k + 1) * width] = part


def mask_amplitudes(live, amp, pair_rows, width):
    tiles = amp.shape[0] // pair_rows
    return pl.pallas_call(
        functools.partial(mask_kernel, pair_rows, width),
        out_shape=pltpu.VMEM(amp.shape, amp.dtype),
        in_specs=[SMEM, HBM],
        out_specs=VMEM,
        scratch_shapes=[pltpu.SemaphoreType.DMA((tiles,))],
        compiler_params=SMALL,
        name="mask",
    )(live, pltpu.with_memory_space_constraint(amp, pltpu.HBM))


def add_tiles(places, total, parts, refs, held_tiles, cols, rows):
    my_row, my_col = lax.axis_index("row"), lax.axis_index("col")
    base, step = places_at(cols), cols // 4

    def add(ref, half, line, q):
        width = ref.shape[1]
        far = q // held_tiles
        row_mask, col_mask = 2 * (line // step) + half, line % step + far * step
        entry = ((my_row ^ row_mask) * cols + (my_col ^ col_mask)) * held_tiles + q % held_tiles
        k, a = places[base + 2 * entry], places[base + 2 * entry + 1]
        inner = pl.ds(pl.multiple_of(k * width, width), width)
        outer = pl.ds(pl.multiple_of(a * width, width), width)
        total[:, outer] += jnp.dot(rows(inner), ref[q * width : (q + 1) * width, :], preferred_element_type=jnp.float32)

    for (half, line), ref in zip(parts, refs):
        for q in range(4 * held_tiles):
            add(ref, half, line, q)


def contract_all_kernel(parts, fresh, held_tiles, cols, table, amp, *rest):
    refs, total = rest[: len(parts)], rest[-1]
    if fresh:
        total[...] = jnp.zeros_like(total)
    add_tiles(table, total, parts, refs, held_tiles, cols, lambda inner: amp[:, inner])


def contract_one_kernel(slot, parts, pair_rows, held_tiles, cols, table, amp, given, *rest):
    refs, (out, _, one) = rest[:-3], rest[-3:]
    picked = pl.ds(pl.multiple_of(table[slot] * pair_rows, pair_rows), pair_rows)
    one[...] = given[picked, :]
    add_tiles(table, one, parts, refs, held_tiles, cols, lambda inner: amp[picked, inner])
    out[...] = one[...].astype(out.dtype)


def contract_rest_kernel(slots, own, parts, pair_rows, held_tiles, cols, table, amp, given, *rest):
    refs, rest = rest[: len(parts)], rest[len(parts) :]
    outs = rest[: len(slots)]
    if own:
        total, ladder, kept, sems = rest[len(slots) :]
    else:
        (total,) = rest[len(slots) :]
    add_tiles(table, total, parts, refs, held_tiles, cols, lambda inner: amp[:, inner])

    def product(slot):
        start = pl.multiple_of(table[slot] * pair_rows, pair_rows)
        return total[pl.ds(start, pair_rows), :]

    copies = []
    for n, (slot, where) in enumerate(own):
        start = pl.multiple_of(jnp.maximum(table[where], 0) * pair_rows, pair_rows)
        kept[n] = product(slot).astype(kept.dtype)
        copy = pltpu.make_async_copy(kept.at[n], ladder.at[pl.ds(start, pair_rows), :], sems.at[n])
        copies.append((table[where] >= 0, copy))
        pl.when(table[where] >= 0)(copy.start)
    for slot, out in zip(slots, outs):
        out[...] = product(slot).astype(out.dtype)
    for there, copy in copies:
        pl.when(there)(copy.wait)


def contract_all(table, amp, gathered, parts, sizes, total=None):
    refs = [gathered[part] for part in parts]
    shape = (amp.shape[0], AT * refs[0].shape[1])
    given = [] if total is None else [total]
    return pl.pallas_call(
        functools.partial(contract_all_kernel, parts, total is None, *sizes[1:]),
        out_shape=pltpu.VMEM(shape, jnp.float32),
        in_specs=[SMEM] + [VMEM] * (1 + len(refs) + len(given)),
        out_specs=VMEM,
        input_output_aliases={2 + len(refs): 0} if given else {},
        compiler_params=GRANT,
        name="contract_all",
    )(table, amp, *refs, *given)


def contract_one(slot, table, amp, gathered, parts, total, sizes):
    refs = [gathered[part] for part in parts]
    shape = (sizes[0], total.shape[1])
    return pl.pallas_call(
        functools.partial(contract_one_kernel, slot, parts, *sizes),
        out_shape=[pltpu.VMEM(shape, amp.dtype), pltpu.VMEM(total.shape, total.dtype)],
        in_specs=[SMEM] + [VMEM] * (2 + len(refs)),
        out_specs=[VMEM, VMEM],
        scratch_shapes=[pltpu.VMEM(shape, jnp.float32)],
        input_output_aliases={2: 1},
        compiler_params=GRANT,
        name="contract_one",
    )(table, amp, total, *refs)


def contract_rest(slots, own, table, amp, gathered, parts, total, sizes):
    refs = [gathered[part] for part in parts]
    shape = (sizes[0], total.shape[1])
    out_shape = [pltpu.VMEM(shape, amp.dtype)] * len(slots)
    out_shape.append(pltpu.VMEM(total.shape, total.dtype))
    scratch = []
    if own:
        out_shape.append(pltpu.HBM(total.shape, amp.dtype))
        scratch = [pltpu.VMEM((len(own), *shape), amp.dtype), pltpu.SemaphoreType.DMA((len(own),))]
    return pl.pallas_call(
        functools.partial(contract_rest_kernel, slots, own, parts, *sizes),
        out_shape=out_shape,
        in_specs=[SMEM] + [VMEM] * (2 + len(refs)),
        out_specs=[VMEM] * (len(slots) + 1) + [HBM] * (1 if own else 0),
        scratch_shapes=scratch,
        input_output_aliases={2: len(slots)},
        compiler_params=GRANT,
        name="contract_rest",
    )(table, amp, total, *refs)


def places_at(cols):
    return 3 * cols + 4


def table_kernel(cols, destination, integrals, table):
    my_col = lax.axis_index("col")
    count = destination.shape[0]
    again, seen_at, base = cols + 4, 2 * cols + 4, places_at(cols)
    for n in range(base):
        table[n] = 0
    table[cols + 2] = -1
    table[cols + 3] = -1
    for s in range(count):
        owner, spot = split(destination[s], count)
        mask = split(owner, cols)[1] ^ my_col
        seen = table[seen_at + mask]
        table[seen_at + mask] = seen + 1

        @pl.when(seen == 0)
        def _(s=s, mask=mask):
            table[mask] = s

        @pl.when(seen > 0)
        def _(s=s, mask=mask):
            table[again + mask] = s

        @pl.when(mask == 0)
        def _(s=s, seen=seen, spot=spot):
            table[cols + 2 + jnp.minimum(seen, 1)] = spot

        @pl.when(jnp.logical_and(mask == 0, seen > 0))
        def _(s=s):
            table[cols] = s

        @pl.when(jnp.logical_and(mask != 0, seen > 0))
        def _(s=s):
            table[cols + 1] = s

    for n in range(integrals.shape[1]):
        table[base + 2 * n] = integrals[0, n]
        table[base + 2 * n + 1] = integrals[1, n]


def make_table(destination, integrals, cols):
    size = places_at(cols) + 2 * integrals.shape[1]
    return pl.pallas_call(
        functools.partial(table_kernel, cols),
        out_shape=pltpu.SMEM((size,), jnp.int32),
        in_specs=[SMEM, SMEM],
        out_specs=SMEM,
        compiler_params=SMALL,
        name="table",
    )(destination, integrals)


def split(value, size):
    if size & (size - 1):
        return lax.div(value, size), lax.rem(value, size)
    return lax.shift_right_logical(value, size.bit_length() - 1), value & (size - 1)


def destinations(ref, far):
    told = ref[pl.ds(ref.shape[0] - META, META), :].astype(jnp.float32)
    return told[2 * far : 2 * far + 1], told[2 * far + 1 : 2 * far + 2]


def arrivals_kernel(slots, *refs):
    my_col = lax.axis_index("col")
    mine, (positions, onward) = refs[:-2], refs[-2:]
    told = [destinations(mine[n], far) for n, far in slots]
    column = jnp.concatenate([t[0] for t in told], axis=0).astype(jnp.int32)
    spot = jnp.concatenate([t[1] for t in told], axis=0).astype(jnp.int32)
    lane = lax.broadcasted_iota(jnp.int32, column.shape, 1)

    def landing(owner):
        match = column == owner
        first = jnp.min(jnp.where(match, lane, NONE), axis=1, keepdims=True)
        match = jnp.logical_and(match, lane != first)
        second = jnp.min(jnp.where(match, lane, NONE), axis=1, keepdims=True)

        def spot_at(at):
            found = jnp.sum(jnp.where(lane == at, spot, 0), axis=1, keepdims=True)
            return jnp.where(at < NONE, found, -1)

        return spot_at(first), spot_at(second)

    first, second = landing(my_col)
    _, passed = landing(my_col ^ 1)
    for m in range(len(slots)):
        positions[m] = first[m, 0]
        positions[len(slots) + m] = second[m, 0]
    chosen, odd = jnp.int32(0), jnp.int32(-1)
    for m in range(2, len(slots), 2):
        chosen = jnp.where(passed[m, 0] >= 0, m, chosen)
    for m in range(1, len(slots), 2):
        odd = jnp.maximum(odd, second[m, 0])
    onward[0] = chosen
    positions[2 * len(slots)] = odd


def arrivals(mine, slots):
    return pl.pallas_call(
        functools.partial(arrivals_kernel, slots),
        out_shape=[
            pltpu.SMEM((2 * len(slots) + 1,), jnp.int32),
            pltpu.SMEM((1,), jnp.int32),
        ],
        in_specs=[VMEM] * len(mine),
        out_specs=[SMEM, SMEM],
        compiler_params=SMALL,
        name="arrivals",
    )(*mine)


def crowding_kernel(groups, *refs):
    my_col = lax.axis_index("col")
    refs, crowded = refs[:-1], refs[-1]
    worst = jnp.int32(0)
    for slots in groups:
        column = [destinations(refs[n], far)[0] for n, far in slots]
        column = jnp.concatenate(column, axis=0)
        column = column.astype(jnp.int32)
        lane = lax.broadcasted_iota(jnp.int32, column.shape, 1)
        owner = lax.broadcasted_iota(jnp.int32, column.shape, 0) ^ my_col
        spare = jnp.zeros(column.shape, jnp.int32)
        for d in range(len(slots)):
            count = jnp.sum((column == d).astype(jnp.int32), axis=1, keepdims=True)
            spare = jnp.where(lane == d, jnp.maximum(count - 1, 0), spare)
        spare = jnp.where(lane == owner, 0, spare)
        sent = jnp.max(jnp.sum(spare, axis=1, keepdims=True))
        taken = jnp.max(jnp.sum(spare, axis=0, keepdims=True))
        worst = jnp.maximum(worst, jnp.maximum(sent, taken))
    crowded[0] = worst


def crowding(blocks, groups):
    return pl.pallas_call(
        functools.partial(crowding_kernel, groups),
        out_shape=jax.ShapeDtypeStruct((1,), jnp.int32),
        in_specs=[VMEM] * len(blocks),
        out_specs=SMEM,
        compiler_params=SMALL,
        name="crowding",
    )(*blocks)


def choose_kernel(onward, *rest):
    choices, out = rest[:-1], rest[-1]
    for n, choice in enumerate(choices):

        @pl.when(onward[0] == 2 * n)
        def _(choice=choice):
            out[...] = choice[...]


def choose(onward, choices):
    return pl.pallas_call(
        choose_kernel,
        out_shape=pltpu.VMEM(choices[0].shape, choices[0].dtype),
        in_specs=[SMEM] + [VMEM] * len(choices),
        out_specs=VMEM,
        compiler_params=SMALL,
        name="choose",
    )(onward, *choices)


def place_kernel(places, positions, *rest):
    sources = rest[: len(places)]
    out, left = rest[-2:]
    rows = sources[0].shape[0]

    def store(n):
        start = pl.multiple_of(jnp.maximum(positions[places[n]], 0) * rows, rows)
        return pltpu.make_async_copy(sources[n], out.at[pl.ds(start, rows), :], left.at[n])

    for n in range(len(places)):
        pl.when(positions[places[n]] >= 0)(lambda n=n: store(n).start())
    for n in range(len(places)):
        pl.when(positions[places[n]] >= 0)(lambda n=n: store(n).wait())


def place(places, positions, sources, ladder):
    count = len(sources)
    return pl.pallas_call(
        functools.partial(place_kernel, places),
        out_shape=pltpu.HBM(ladder.shape, ladder.dtype),
        in_specs=[SMEM] + [VMEM] * count + [HBM],
        out_specs=HBM,
        scratch_shapes=[pltpu.SemaphoreType.DMA((count,))],
        input_output_aliases={1 + count: 0},
        compiler_params=SMALL,
        name="place",
    )(positions, *sources, ladder)


def shards(sizes, *arrays):
    return step(sizes, *arrays)


def hops(cols):
    high = [1 << b for b in reversed(range(1, cols.bit_length() - 1))]
    far = [(None, m) for m in reversed(range(high[0], cols))]
    near = [(None, m) for m in reversed(range(1, high[0]))]
    late, known = [], [0]
    for bit in high:
        late += [(m, bit) for m in known if m]
        known += [m | bit for m in known]
    order = [(0, bit) for bit in high] + far[:1] + near[-1:] + late
    rest = []
    for n, hop in enumerate(far[1:]):
        rest += [hop] + near[:-1][n : n + 1]
    return order + rest[:-1] + [LAST] + rest[-1:]


def step(sizes, amplitudes, live_tiles, destination, integral_list, integral_tiles):
    rows, cols = sizes
    tile_count = destination.shape[0]
    pair_rows = amplitudes.shape[0] // tile_count
    held_tiles, width, _ = integral_tiles.shape
    masked = mask_amplitudes(live_tiles, amplitudes, pair_rows, width)
    gathered, came = gather_all(make_block(destination, integral_tiles, cols), sizes)
    table = make_table(destination, integral_list.T, cols)
    shape = (pair_rows, held_tiles, cols)
    soon, late = came[: len(came) // 2], came[len(came) // 2 :]
    total = contract_all(table, masked, gathered, [(0, n) for n in soon], shape)
    parts = [(0, n) for n in late] + [(1, n) for n in soon]
    total = contract_all(table, masked, gathered, parts, shape, total)
    parts = [(1, n) for n in late]
    extra_tile, total = contract_one(cols + 1, table, masked, gathered, parts, total, shape)
    slots = list(range(1, cols))
    own = [(0, cols + 2), (cols, cols + 3)]
    *outs, _, ladder = contract_rest(slots, own, table, masked, gathered, parts, total, shape)

    held = [gather_mask(q, half, cols) for half in (0, 1) for q in range(rows * cols // 2)]
    index = {m: (n // 4, n % 4) for n, m in enumerate(held)}
    groups = [[index[(r, c)] for c in range(cols)] for r in range(rows)]
    order = sorted(came)
    positions, onward = arrivals([gathered[0, n] for n in order], groups[0])
    crowded = crowding([gathered[h, n] for h in (0, 1) for n in order], groups)

    evens = list(range(2, cols, 2))
    carried, direct = {0: extra_tile}, {}
    for hop in hops(cols):
        m, bit = hop
        if hop == LAST:
            last = choose(onward, [carried[0]] + [carried[m] for m in evens])
            last = local(swap(last, (0, 1), sizes))
        elif m is None:
            direct[bit] = local(swap(outs[bit - 1], (0, bit), sizes))
        else:
            carried[m | bit] = local(swap(carried[m], (0, bit), sizes))

    order = [m for c, m in hops(cols) if c is None and m]
    soon, late = order[:-2], order[-2:]
    spots = soon + [cols + m for m in evens] + [2 * cols]
    sources = [direct[m] for m in soon] + [carried[m] for m in evens] + [last]
    ladder = place(spots, positions, sources, ladder)

    def again(state):
        return state[0] > 1

    def send_seconds(state):
        masked = mask_amplitudes(live_tiles, amplitudes, pair_rows, width)
        gathered, came = gather_all(make_block(destination, integral_tiles, cols), sizes)
        table = make_table(destination, integral_list.T, cols)
        parts = [(0, n) for n in came]
        total = contract_all(table, masked, gathered, parts, shape)
        again = [cols + 4 + m for m in slots]
        parts = [(1, n) for n in came]
        *outs, _ = contract_rest(again, [], table, masked, gathered, parts, total, shape)
        outs = [local(swap(out, (0, m), sizes)) for m, out in zip(slots, outs)]
        spots = list(range(cols + 1, 2 * cols))
        return jnp.zeros_like(state[0]), place(spots, positions, outs, state[1])

    ladder = lax.while_loop(again, send_seconds, (crowded[0], ladder))[1]

    return place(late, positions, [direct[m] for m in late], ladder)


def solution(mesh):
    in_specs = (
        P(("row", "col"), None),
        P(("row", "col"), None),
        P(("row", "col")),
        P(),
        P(("row", "col"), None, None),
    )
    out_specs = P(("row", "col"), None)
    body = functools.partial(shards, (mesh.shape["row"], mesh.shape["col"]))
    return jax.shard_map(body, mesh=mesh, in_specs=in_specs, out_specs=out_specs, check_vma=False)
```

```python
import functools

import jax
import jax.numpy as jnp
from jax import lax
from jax.experimental import pallas as pl
from jax.experimental.pallas import tpu as pltpu
from jax.sharding import PartitionSpec as P


AT = 8


GRANT = pltpu.CompilerParams(vmem_limit_bytes=40 * 1024 * 1024)
SMALL = pltpu.CompilerParams(vmem_limit_bytes=12 * 1024 * 1024)
VMEM = pl.BlockSpec(memory_space=pltpu.VMEM)
SMEM = pl.BlockSpec(memory_space=pltpu.SMEM)
ANY = pl.BlockSpec(memory_space=pl.ANY)
HBM = pl.BlockSpec(memory_space=pltpu.HBM)
LAST = (None, None)
NONE = 1 << 20
META = 16


def swap(value, mask, sizes):
    rows, cols = sizes
    pairs = [
        (r * cols + c, (r ^ mask[0]) * cols + (c ^ mask[1]))
        for r in range(rows)
        for c in range(cols)
    ]
    return lax.ppermute(value, ("row", "col"), pairs)


def local(value):
    return pltpu.with_memory_space_constraint(value, pltpu.VMEM)


def block_kernel(cols, destination, integrals, out, rows):
    held, width, _ = integrals.shape
    tiles = destination.shape[1]
    rows[...] = jnp.full(rows.shape, -1.0, rows.dtype)
    owner, spot = split(destination[...], tiles)
    rows[0:1, :tiles] = split(owner, cols)[1].astype(rows.dtype)
    rows[1:2, :tiles] = spot.astype(rows.dtype)
    for t in range(held):
        out[t, :width, :] = integrals[t]
        out[t, width:, :] = rows[...].astype(out.dtype)


def make_block(destination, integrals, cols):
    held, width, _ = integrals.shape
    return pl.pallas_call(
        functools.partial(block_kernel, cols),
        out_shape=pltpu.VMEM((held, width + META, width), integrals.dtype),
        in_specs=[VMEM, VMEM],
        out_specs=VMEM,
        scratch_shapes=[pltpu.VMEM((META, width), jnp.float32)],
        compiler_params=SMALL,
        name="block",
    )(destination[None], integrals)


def join_kernel(*refs):
    pieces, out, rows = refs[:4], refs[4], refs[5]
    held, _, width = pieces[0].shape
    rows[...] = jnp.full(rows.shape, -1.0, rows.dtype)
    for n, piece in enumerate(pieces):
        for t in range(held):
            start = (n * held + t) * width
            out[start : start + width, :] = piece[t, :width, :]
        told = piece[0, width:, :].astype(rows.dtype)
        rows[2 * n : 2 * n + 2, :] = told[0:2]
    out[4 * held * width :, :] = rows[...].astype(out.dtype)


def join(pieces):
    held, _, width = pieces[0].shape
    return pl.pallas_call(
        join_kernel,
        out_shape=pltpu.VMEM((4 * held * width + META, width), pieces[0].dtype),
        in_specs=[VMEM] * 4,
        out_specs=VMEM,
        scratch_shapes=[pltpu.VMEM((META, width), jnp.float32)],
        compiler_params=SMALL,
        name="join",
    )(*[local(x) for x in pieces])


def gather_all(block, sizes):
    rows, cols = sizes
    step = cols // 4
    near = [(2 * i, j) for i in range(rows // 2) for j in range(step)]
    pieces = {0: block}
    for m in (3, 2, 1):
        pieces[m] = swap(block, (0, m * step), sizes)
    line = join([pieces[m] for m in range(4)])
    mine, other = {0: line}, {}
    for n in reversed(range(1, len(near))):
        mine[n] = swap(line, near[n], sizes)
    for n in mine:
        other[n] = swap(mine[n], (1, 0), sizes)
    gathered = {(0, n): local(mine[n]) for n in mine}
    gathered.update({(1, n): local(other[n]) for n in other})
    return gathered, list(mine)


def gather_mask(q, half, cols):
    step = cols // 4
    line, far = divmod(q, 4)
    return 2 * (line // step) + half, line % step + far * step


def mask_kernel(pair_rows, width, live, amp, out, sems):
    tiles = amp.shape[0] // pair_rows

    def fetch(s):
        rows = pl.ds(s * pair_rows, pair_rows)
        return pltpu.make_async_copy(amp.at[rows, :], out.at[rows, :], sems.at[s])

    for s in range(tiles):
        fetch(s).start()
    for s in range(tiles):
        fetch(s).wait()
        for k in range(amp.shape[1] // width):
            part = out[s * pair_rows : (s + 1) * pair_rows, k * width : (k + 1) * width]
            part = jnp.where(live[s, k] != 0, part, jnp.zeros_like(part))
            out[s * pair_rows : (s + 1) * pair_rows, k * width : (k + 1) * width] = part


def mask_amplitudes(live, amp, pair_rows, width):
    tiles = amp.shape[0] // pair_rows
    return pl.pallas_call(
        functools.partial(mask_kernel, pair_rows, width),
        out_shape=pltpu.VMEM(amp.shape, amp.dtype),
        in_specs=[SMEM, HBM],
        out_specs=VMEM,
        scratch_shapes=[pltpu.SemaphoreType.DMA((tiles,))],
        compiler_params=SMALL,
        name="mask",
    )(live, pltpu.with_memory_space_constraint(amp, pltpu.HBM))


def add_tiles(places, total, parts, refs, held_tiles, cols, rows):
    my_row, my_col = lax.axis_index("row"), lax.axis_index("col")
    base, step = places_at(cols), cols // 4

    def add(ref, half, line, q):
        width = ref.shape[1]
        far = q // held_tiles
        row_mask, col_mask = 2 * (line // step) + half, line % step + far * step
        entry = ((my_row ^ row_mask) * cols + (my_col ^ col_mask)) * held_tiles + q % held_tiles
        k, a = places[base + 2 * entry], places[base + 2 * entry + 1]
        inner = pl.ds(pl.multiple_of(k * width, width), width)
        outer = pl.ds(pl.multiple_of(a * width, width), width)
        total[:, outer] += jnp.dot(rows(inner), ref[q * width : (q + 1) * width, :], preferred_element_type=jnp.float32)

    for (half, line), ref in zip(parts, refs):
        for q in range(4 * held_tiles):
            add(ref, half, line, q)


def contract_all_kernel(parts, fresh, held_tiles, cols, table, amp, *rest):
    refs, total = rest[: len(parts)], rest[-1]
    if fresh:
        total[...] = jnp.zeros_like(total)
    add_tiles(table, total, parts, refs, held_tiles, cols, lambda inner: amp[:, inner])


def contract_one_kernel(slot, parts, pair_rows, held_tiles, cols, table, amp, given, *rest):
    refs, (out, _, one) = rest[:-3], rest[-3:]
    picked = pl.ds(pl.multiple_of(table[slot] * pair_rows, pair_rows), pair_rows)
    one[...] = given[picked, :]
    add_tiles(table, one, parts, refs, held_tiles, cols, lambda inner: amp[picked, inner])
    out[...] = one[...].astype(out.dtype)


def contract_rest_kernel(slots, own, parts, pair_rows, held_tiles, cols, table, amp, given, *rest):
    refs, rest = rest[: len(parts)], rest[len(parts) :]
    outs = rest[: len(slots)]
    if own:
        total, ladder, kept, sems = rest[len(slots) :]
    else:
        (total,) = rest[len(slots) :]
    add_tiles(table, total, parts, refs, held_tiles, cols, lambda inner: amp[:, inner])

    def product(slot):
        start = pl.multiple_of(table[slot] * pair_rows, pair_rows)
        return total[pl.ds(start, pair_rows), :]

    copies = []
    for n, (slot, where) in enumerate(own):
        start = pl.multiple_of(jnp.maximum(table[where], 0) * pair_rows, pair_rows)
        kept[n] = product(slot).astype(kept.dtype)
        copy = pltpu.make_async_copy(kept.at[n], ladder.at[pl.ds(start, pair_rows), :], sems.at[n])
        copies.append((table[where] >= 0, copy))
        pl.when(table[where] >= 0)(copy.start)
    for slot, out in zip(slots, outs):
        out[...] = product(slot).astype(out.dtype)
    for there, copy in copies:
        pl.when(there)(copy.wait)


def contract_all(table, amp, gathered, parts, sizes, total=None):
    refs = [gathered[part] for part in parts]
    shape = (amp.shape[0], AT * refs[0].shape[1])
    given = [] if total is None else [total]
    return pl.pallas_call(
        functools.partial(contract_all_kernel, parts, total is None, *sizes[1:]),
        out_shape=pltpu.VMEM(shape, jnp.float32),
        in_specs=[SMEM] + [VMEM] * (1 + len(refs) + len(given)),
        out_specs=VMEM,
        input_output_aliases={2 + len(refs): 0} if given else {},
        compiler_params=GRANT,
        name="contract_all",
    )(table, amp, *refs, *given)


def contract_one(slot, table, amp, gathered, parts, total, sizes):
    refs = [gathered[part] for part in parts]
    shape = (sizes[0], total.shape[1])
    return pl.pallas_call(
        functools.partial(contract_one_kernel, slot, parts, *sizes),
        out_shape=[pltpu.VMEM(shape, amp.dtype), pltpu.VMEM(total.shape, total.dtype)],
        in_specs=[SMEM] + [VMEM] * (2 + len(refs)),
        out_specs=[VMEM, VMEM],
        scratch_shapes=[pltpu.VMEM(shape, jnp.float32)],
        input_output_aliases={2: 1},
        compiler_params=GRANT,
        name="contract_one",
    )(table, amp, total, *refs)


def contract_rest(slots, own, table, amp, gathered, parts, total, sizes):
    refs = [gathered[part] for part in parts]
    shape = (sizes[0], total.shape[1])
    out_shape = [pltpu.VMEM(shape, amp.dtype)] * len(slots)
    out_shape.append(pltpu.VMEM(total.shape, total.dtype))
    scratch = []
    if own:
        out_shape.append(pltpu.HBM(total.shape, amp.dtype))
        scratch = [pltpu.VMEM((len(own), *shape), amp.dtype), pltpu.SemaphoreType.DMA((len(own),))]
    return pl.pallas_call(
        functools.partial(contract_rest_kernel, slots, own, parts, *sizes),
        out_shape=out_shape,
        in_specs=[SMEM] + [VMEM] * (2 + len(refs)),
        out_specs=[VMEM] * (len(slots) + 1) + [HBM] * (1 if own else 0),
        scratch_shapes=scratch,
        input_output_aliases={2: len(slots)},
        compiler_params=GRANT,
        name="contract_rest",
    )(table, amp, total, *refs)


def places_at(cols):
    return 3 * cols + 4


def table_kernel(cols, destination, integrals, table):
    my_col = lax.axis_index("col")
    count = destination.shape[0]
    again, seen_at, base = cols + 4, 2 * cols + 4, places_at(cols)
    for n in range(base):
        table[n] = 0
    table[cols + 2] = -1
    table[cols + 3] = -1
    for s in range(count):
        owner, spot = split(destination[s], count)
        mask = split(owner, cols)[1] ^ my_col
        seen = table[seen_at + mask]
        table[seen_at + mask] = seen + 1

        @pl.when(seen == 0)
        def _(s=s, mask=mask):
            table[mask] = s

        @pl.when(seen > 0)
        def _(s=s, mask=mask):
            table[again + mask] = s

        @pl.when(mask == 0)
        def _(s=s, seen=seen, spot=spot):
            table[cols + 2 + jnp.minimum(seen, 1)] = spot

        @pl.when(jnp.logical_and(mask == 0, seen > 0))
        def _(s=s):
            table[cols] = s

        @pl.when(jnp.logical_and(mask != 0, seen > 0))
        def _(s=s):
            table[cols + 1] = s

    for n in range(integrals.shape[1]):
        table[base + 2 * n] = integrals[0, n]
        table[base + 2 * n + 1] = integrals[1, n]


def make_table(destination, integrals, cols):
    size = places_at(cols) + 2 * integrals.shape[1]
    return pl.pallas_call(
        functools.partial(table_kernel, cols),
        out_shape=pltpu.SMEM((size,), jnp.int32),
        in_specs=[SMEM, SMEM],
        out_specs=SMEM,
        compiler_params=SMALL,
        name="table",
    )(destination, integrals)


def split(value, size):
    if size & (size - 1):
        return lax.div(value, size), lax.rem(value, size)
    return lax.shift_right_logical(value, size.bit_length() - 1), value & (size - 1)


def destinations(ref, far):
    told = ref[pl.ds(ref.shape[0] - META, META), :].astype(jnp.float32)
    return told[2 * far : 2 * far + 1], told[2 * far + 1 : 2 * far + 2]


def arrivals_kernel(slots, *refs):
    my_col = lax.axis_index("col")
    mine, (positions, onward) = refs[:-2], refs[-2:]
    told = [destinations(mine[n], far) for n, far in slots]
    column = jnp.concatenate([t[0] for t in told], axis=0).astype(jnp.int32)
    spot = jnp.concatenate([t[1] for t in told], axis=0).astype(jnp.int32)
    lane = lax.broadcasted_iota(jnp.int32, column.shape, 1)

    def landing(owner):
        match = column == owner
        first = jnp.min(jnp.where(match, lane, NONE), axis=1, keepdims=True)
        match = jnp.logical_and(match, lane != first)
        second = jnp.min(jnp.where(match, lane, NONE), axis=1, keepdims=True)

        def spot_at(at):
            found = jnp.sum(jnp.where(lane == at, spot, 0), axis=1, keepdims=True)
            return jnp.where(at < NONE, found, -1)

        return spot_at(first), spot_at(second)

    first, second = landing(my_col)
    _, passed = landing(my_col ^ 1)
    for m in range(len(slots)):
        positions[m] = first[m, 0]
        positions[len(slots) + m] = second[m, 0]
    chosen, odd = jnp.int32(0), jnp.int32(-1)
    for m in range(2, len(slots), 2):
        chosen = jnp.where(passed[m, 0] >= 0, m, chosen)
    for m in range(1, len(slots), 2):
        odd = jnp.maximum(odd, second[m, 0])
    onward[0] = chosen
    positions[2 * len(slots)] = odd


def arrivals(mine, slots):
    return pl.pallas_call(
        functools.partial(arrivals_kernel, slots),
        out_shape=[
            pltpu.SMEM((2 * len(slots) + 1,), jnp.int32),
            pltpu.SMEM((1,), jnp.int32),
        ],
        in_specs=[VMEM] * len(mine),
        out_specs=[SMEM, SMEM],
        compiler_params=SMALL,
        name="arrivals",
    )(*mine)


def crowding_kernel(groups, *refs):
    my_col = lax.axis_index("col")
    refs, crowded = refs[:-1], refs[-1]
    worst = jnp.int32(0)
    for slots in groups:
        column = [destinations(refs[n], far)[0] for n, far in slots]
        column = jnp.concatenate(column, axis=0)
        column = column.astype(jnp.int32)
        lane = lax.broadcasted_iota(jnp.int32, column.shape, 1)
        owner = lax.broadcasted_iota(jnp.int32, column.shape, 0) ^ my_col
        spare = jnp.zeros(column.shape, jnp.int32)
        for d in range(len(slots)):
            count = jnp.sum((column == d).astype(jnp.int32), axis=1, keepdims=True)
            spare = jnp.where(lane == d, jnp.maximum(count - 1, 0), spare)
        spare = jnp.where(lane == owner, 0, spare)
        sent = jnp.max(jnp.sum(spare, axis=1, keepdims=True))
        taken = jnp.max(jnp.sum(spare, axis=0, keepdims=True))
        worst = jnp.maximum(worst, jnp.maximum(sent, taken))
    crowded[0] = worst


def crowding(blocks, groups):
    return pl.pallas_call(
        functools.partial(crowding_kernel, groups),
        out_shape=jax.ShapeDtypeStruct((1,), jnp.int32),
        in_specs=[VMEM] * len(blocks),
        out_specs=SMEM,
        compiler_params=SMALL,
        name="crowding",
    )(*blocks)


def choose_kernel(onward, *rest):
    choices, out = rest[:-1], rest[-1]
    for n, choice in enumerate(choices):

        @pl.when(onward[0] == 2 * n)
        def _(choice=choice):
            out[...] = choice[...]


def choose(onward, choices):
    return pl.pallas_call(
        choose_kernel,
        out_shape=pltpu.VMEM(choices[0].shape, choices[0].dtype),
        in_specs=[SMEM] + [VMEM] * len(choices),
        out_specs=VMEM,
        compiler_params=SMALL,
        name="choose",
    )(onward, *choices)


def place_kernel(places, positions, *rest):
    sources = rest[: len(places)]
    out, left = rest[-2:]
    rows = sources[0].shape[0]

    def store(n):
        start = pl.multiple_of(jnp.maximum(positions[places[n]], 0) * rows, rows)
        return pltpu.make_async_copy(sources[n], out.at[pl.ds(start, rows), :], left.at[n])

    for n in range(len(places)):
        pl.when(positions[places[n]] >= 0)(lambda n=n: store(n).start())
    for n in range(len(places)):
        pl.when(positions[places[n]] >= 0)(lambda n=n: store(n).wait())


def place(places, positions, sources, ladder):
    count = len(sources)
    return pl.pallas_call(
        functools.partial(place_kernel, places),
        out_shape=pltpu.HBM(ladder.shape, ladder.dtype),
        in_specs=[SMEM] + [VMEM] * count + [HBM],
        out_specs=HBM,
        scratch_shapes=[pltpu.SemaphoreType.DMA((count,))],
        input_output_aliases={1 + count: 0},
        compiler_params=SMALL,
        name="place",
    )(positions, *sources, ladder)


def shards(sizes, *arrays):
    return step(sizes, *arrays)


def hops(cols):
    high = [1 << b for b in reversed(range(1, cols.bit_length() - 1))]
    far = [(None, m) for m in reversed(range(high[0], cols))]
    near = [(None, m) for m in reversed(range(1, high[0]))]
    late, known = [], [0]
    for bit in high:
        late += [(m, bit) for m in known if m]
        known += [m | bit for m in known]
    order = [(0, bit) for bit in high] + far[:1] + near[-1:] + late
    rest = []
    for n, hop in enumerate(far[1:]):
        rest += [hop] + near[:-1][n : n + 1]
    return order + rest[:-1] + [LAST] + rest[-1:]


def step(sizes, amplitudes, live_tiles, destination, integral_list, integral_tiles):
    rows, cols = sizes
    tile_count = destination.shape[0]
    pair_rows = amplitudes.shape[0] // tile_count
    held_tiles, width, _ = integral_tiles.shape
    masked = mask_amplitudes(live_tiles, amplitudes, pair_rows, width)
    gathered, came = gather_all(make_block(destination, integral_tiles, cols), sizes)
    table = make_table(destination, integral_list.T, cols)
    shape = (pair_rows, held_tiles, cols)
    steps = [came[:1], came[1 : len(came) // 2], came[len(came) // 2 : -1], came[-1:]]
    total = None
    for mine, theirs in (
        (steps[0], steps[0]), (steps[1], steps[1]), (steps[2] + steps[3], steps[2])
    ):
        parts = [(0, n) for n in mine] + [(1, n) for n in theirs]
        total = contract_all(table, masked, gathered, parts, shape, total)
    parts = [(1, n) for n in steps[3]]
    extra_tile, total = contract_one(cols + 1, table, masked, gathered, parts, total, shape)
    slots = list(range(1, cols))
    own = [(0, cols + 2), (cols, cols + 3)]
    *outs, _, ladder = contract_rest(slots, own, table, masked, gathered, parts, total, shape)

    held = [gather_mask(q, half, cols) for half in (0, 1) for q in range(rows * cols // 2)]
    index = {m: (n // 4, n % 4) for n, m in enumerate(held)}
    groups = [[index[(r, c)] for c in range(cols)] for r in range(rows)]
    order = sorted(came)
    positions, onward = arrivals([gathered[0, n] for n in order], groups[0])
    crowded = crowding([gathered[h, n] for h in (0, 1) for n in order], groups)

    evens = list(range(2, cols, 2))
    carried, direct = {0: extra_tile}, {}
    for hop in hops(cols):
        m, bit = hop
        if hop == LAST:
            last = choose(onward, [carried[0]] + [carried[m] for m in evens])
            last = local(swap(last, (0, 1), sizes))
        elif m is None:
            direct[bit] = local(swap(outs[bit - 1], (0, bit), sizes))
        else:
            carried[m | bit] = local(swap(carried[m], (0, bit), sizes))

    order = [m for c, m in hops(cols) if c is None and m]
    soon, late = order[:-2], order[-2:]
    spots = soon + [cols + m for m in evens] + [2 * cols]
    sources = [direct[m] for m in soon] + [carried[m] for m in evens] + [last]
    ladder = place(spots, positions, sources, ladder)

    def again(state):
        return state[0] > 1

    def send_seconds(state):
        masked = mask_amplitudes(live_tiles, amplitudes, pair_rows, width)
        gathered, came = gather_all(make_block(destination, integral_tiles, cols), sizes)
        table = make_table(destination, integral_list.T, cols)
        parts = [(0, n) for n in came]
        total = contract_all(table, masked, gathered, parts, shape)
        again = [cols + 4 + m for m in slots]
        parts = [(1, n) for n in came]
        *outs, _ = contract_rest(again, [], table, masked, gathered, parts, total, shape)
        outs = [local(swap(out, (0, m), sizes)) for m, out in zip(slots, outs)]
        spots = list(range(cols + 1, 2 * cols))
        return jnp.zeros_like(state[0]), place(spots, positions, outs, state[1])

    ladder = lax.while_loop(again, send_seconds, (crowded[0], ladder))[1]

    return place(late, positions, [direct[m] for m in late], ladder)


def solution(mesh):
    in_specs = (
        P(("row", "col"), None),
        P(("row", "col"), None),
        P(("row", "col")),
        P(),
        P(("row", "col"), None, None),
    )
    out_specs = P(("row", "col"), None)
    body = functools.partial(shards, (mesh.shape["row"], mesh.shape["col"]))
    return jax.shard_map(body, mesh=mesh, in_specs=in_specs, out_specs=out_specs, check_vma=False)
```
